32 devices in a mesh: req: 16 (over z, y, core), tp: 2 (over x).
Axes of the slice: x: 2, y: 2, z: 4, core: 2. Of those that a mesh axis runs over, the one named last changes fastest.
Arguments:
- queries: bfloat16 [96, 24, 8192], P('req', None, 'tp'), may hold values from -8 to 8
- fresh_kv: bfloat16 [96, 24, 2048], P('req', None, 'tp'), may hold values from -8 to 8
- key_value_pages: bfloat16 [832, 128, 2048], P('req', None, 'tp'), may hold values from -6 to 6
- cache_lengths: int32 [96], P('req'), may hold values from 1 to 4096, as said below
- page_table: int32 [96, 32], P('req'), may hold values from 0 to 51, as said below
- movers: int32 [16, 2], P('req'), may hold values from 0 to 5, as said below
- w_out: bfloat16 [4096, 8192], P('req', 'tp'), may hold values from -0.0625 to 0.0625
Outputs:
- projected: bfloat16 [2304, 4096], P('req', 'tp')
The draws below stay inside these ranges and needn't reach their ends.
Inputs may be any that keep to these rules, and one draw needn't show every extreme that they name: `cache_lengths`: in every draw one request holds exactly 4096 positions. `cache_lengths`: A request in a slot named by movers holds at most 512 positions, and in every draw one of them holds exactly that many. `page_table`: the entries that a request's length uses are distinct pages among all requests of its owner; the other entries are any pages of the pool. `movers`: the two slots of a row differ.
All inputs are finite; a program needn't handle non-finite values.
Results may differ from the reference program's by a relative error of at most 0.0057.
Values may be sent and summed in bfloat16 or wider, within the bound.
A program may use at most 320 MiB of HBM per device.

```python
import jax
import jax.numpy as jnp
from jax import lax

QUERY_HEADS = 64
KEY_VALUE_HEADS = 8
HEAD_SIZE = 128
DOUT = 4096
NEW_TOKENS = 24
PAGE_POSITIONS = 128
MAXP = 32
MIGP = 4
REQ_DEV = 6
OWNING_DEVICES = 16
TOTAL_REQUESTS = 96
PAGES_PER_DEVICE = 52
TOKENS = 2304


def layout(key):
    base_key = jax.random.fold_in(key, 11)
    keys_all = jax.random.split(base_key, 7)
    to_next = jax.random.randint(keys_all[0], (OWNING_DEVICES,), 0, REQ_DEV)
    to_prev = (to_next + 1 + jax.random.randint(keys_all[1], (OWNING_DEVICES,), 0, REQ_DEV - 1)) % REQ_DEV
    slot_ids = jnp.arange(REQ_DEV, dtype=jnp.int32)[None, :]
    device = jnp.arange(OWNING_DEVICES, dtype=jnp.int32)[:, None]
    moving = (slot_ids == to_next[:, None]) | (slot_ids == to_prev[:, None])
    exponent = jax.random.randint(keys_all[2], (OWNING_DEVICES, REQ_DEV), 0, 6)
    span = jnp.power(2, exponent)
    wanted = jax.random.randint(keys_all[3], (OWNING_DEVICES, REQ_DEV), 1, span + 1)
    long_owner = jax.random.randint(keys_all[4], (), 0, OWNING_DEVICES)
    short_owner = jax.random.randint(keys_all[5], (), 0, OWNING_DEVICES)
    first_stay = jnp.argmax(jnp.logical_not(moving).astype(jnp.int32), axis=1)
    long_slot = (device == long_owner) & (slot_ids == first_stay[:, None])
    short_slot = (device == short_owner) & (slot_ids == to_next[:, None])
    wanted = jnp.where(long_slot, MAXP, wanted)
    wanted = jnp.where(short_slot, MIGP, wanted)
    wanted = jnp.minimum(wanted, jnp.where(moving, MIGP, MAXP))
    ranking = slot_ids + REQ_DEV * jnp.logical_not(moving).astype(jnp.int32)
    ordering = jnp.argsort(ranking, axis=1)
    remaining = jnp.full((OWNING_DEVICES,), PAGES_PER_DEVICE, dtype=jnp.int32)
    page_list = jnp.zeros((OWNING_DEVICES, REQ_DEV), dtype=jnp.int32)
    owner_ids = jnp.arange(OWNING_DEVICES, dtype=jnp.int32)
    for position in range(REQ_DEV):
        chosen = ordering[:, position]
        want_here = jnp.take_along_axis(wanted, chosen[:, None], axis=1)[:, 0]
        granted = jnp.minimum(want_here, remaining - (REQ_DEV - 1 - position))
        page_list = page_list.at[owner_ids, chosen].set(granted)
        remaining = remaining - granted
    tail = jax.random.randint(keys_all[6], (OWNING_DEVICES, REQ_DEV), 1, PAGE_POSITIONS + 1)
    tail = jnp.where(long_slot | short_slot, PAGE_POSITIONS, tail)
    lengths = (page_list - 1) * PAGE_POSITIONS + tail
    return (to_next, to_prev, page_list, lengths)


def draw_movers(key, part):
    to_next, to_prev, page_list, lengths = layout(key)
    return jnp.stack([to_next, to_prev], axis=1).astype(jnp.int32)


def draw_cache_lengths(key, part):
    to_next, to_prev, page_list, lengths = layout(key)
    return lengths.reshape(TOTAL_REQUESTS).astype(jnp.int32)


def draw_page_table(key, part):
    to_next, to_prev, page_list, lengths = layout(key)
    table_key = jax.random.fold_in(key, 23)
    key_perm, key_fill = jax.random.split(table_key)
    shuffles = jax.vmap(lambda single: jax.random.permutation(single, PAGES_PER_DEVICE))(jax.random.split(key_perm, OWNING_DEVICES))
    start = jnp.cumsum(page_list, axis=1) - page_list
    column = jnp.arange(MAXP, dtype=jnp.int32)[None, None, :]
    where_from = jnp.minimum(start[:, :, None] + column, PAGES_PER_DEVICE - 1).reshape(OWNING_DEVICES, REQ_DEV * MAXP)
    picked = jnp.take_along_axis(shuffles, where_from, axis=1).reshape(OWNING_DEVICES, REQ_DEV, MAXP)
    filler = jax.random.randint(key_fill, (OWNING_DEVICES, REQ_DEV, MAXP), 0, PAGES_PER_DEVICE)
    table = jnp.where(column < page_list[:, :, None], picked, filler)
    return table.reshape(TOTAL_REQUESTS, MAXP).astype(jnp.int32)


def draw_queries(key, part):
    own_random_key = jax.random.fold_in(key, 41)
    value_rows = jnp.clip(jax.random.normal(own_random_key, (TOTAL_REQUESTS, NEW_TOKENS, QUERY_HEADS * HEAD_SIZE), jnp.float32), -6.0, 6.0)
    return value_rows.astype(jnp.bfloat16)


def draw_fresh_kv(key, part):
    own_random_key = jax.random.fold_in(key, 43)
    value_rows = jnp.clip(jax.random.normal(own_random_key, (TOTAL_REQUESTS, NEW_TOKENS, KEY_VALUE_HEADS, 2, HEAD_SIZE), jnp.float32), -6.0, 6.0)
    return value_rows.reshape(TOTAL_REQUESTS, NEW_TOKENS, KEY_VALUE_HEADS * 2 * HEAD_SIZE).astype(jnp.bfloat16)


def block_scale(own_key, shape, shards, low, largest):
    loudness, own = 1.0, jax.random.fold_in(own_key, 6)
    for axis_at, blocks in shards:
        heights = jnp.exp(jax.random.uniform(jax.random.fold_in(own, axis_at), (blocks,), jnp.float32, low / len(shards), largest / len(shards)))
        loudness = loudness * jnp.repeat(heights, shape[axis_at] // blocks).reshape([-1 if axis == axis_at else 1 for axis in range(len(shape))])
    return loudness


def normal_values(own_key, shape, spread, bound, cuts=(), held_as=jnp.bfloat16):
    level = block_scale(own_key, shape, cuts, -0.22, 0.18) if cuts else 1.0
    values = jax.random.normal(own_key, shape, jnp.float32) * spread * level
    return jnp.minimum(jnp.maximum(values, -bound), bound).astype(held_as)


def setup_inputs(seed: int = 0) -> dict:
    streams_of = jax.random.split(jax.random.key(seed), 8)
    return {
        "queries": draw_queries(jax.random.fold_in(streams_of[7], 71), 0),
        "fresh_kv": draw_fresh_kv(jax.random.fold_in(streams_of[7], 71), 0),
        "key_value_pages": normal_values(streams_of[2], (OWNING_DEVICES * PAGES_PER_DEVICE, PAGE_POSITIONS, KEY_VALUE_HEADS * 2 * HEAD_SIZE), 1.0, 6.0, ((0, 16), (2, 2))),
        "cache_lengths": draw_cache_lengths(jax.random.fold_in(streams_of[7], 71), 0),
        "page_table": draw_page_table(jax.random.fold_in(streams_of[7], 71), 0),
        "movers": draw_movers(jax.random.fold_in(streams_of[7], 71), 0),
        "w_out": normal_values(streams_of[6], (DOUT, QUERY_HEADS * HEAD_SIZE), (QUERY_HEADS * HEAD_SIZE) ** -0.5, 0.0625, ((0, 16), (1, 2))),
    }


masked_score = -1e30


def attend_one(query_rows, fresh_rows, page_list, length):
    cached_rows = MAXP * PAGE_POSITIONS
    query_head_rows = query_rows.astype(jnp.float32).reshape(NEW_TOKENS, KEY_VALUE_HEADS, QUERY_HEADS // KEY_VALUE_HEADS, HEAD_SIZE)
    cache_block = page_list.astype(jnp.float32).reshape(cached_rows, KEY_VALUE_HEADS, 2, HEAD_SIZE)
    newer_rows = fresh_rows.astype(jnp.float32).reshape(NEW_TOKENS, KEY_VALUE_HEADS, 2, HEAD_SIZE)
    all_keys = jnp.concatenate([cache_block[:, :, 0], newer_rows[:, :, 0]], axis=0)
    all_values = jnp.concatenate([cache_block[:, :, 1], newer_rows[:, :, 1]], axis=0)
    scores = jnp.einsum("qkgd,ckd->kgqc", query_head_rows, all_keys) * (HEAD_SIZE ** -0.5)
    position = jnp.arange(cached_rows + NEW_TOKENS, dtype=jnp.int32)[None, :]
    token_row = jnp.arange(NEW_TOKENS, dtype=jnp.int32)[:, None]
    valid = jnp.where(position < cached_rows, position < length, position - cached_rows <= token_row)
    scores = jnp.where(valid, scores, masked_score)
    highest = jnp.max(scores, axis=-1, keepdims=True)
    powers = jnp.exp(scores - highest)
    weights = (powers / jnp.sum(powers, axis=-1, keepdims=True)).astype(jnp.bfloat16)
    mixed = jnp.einsum("kgqc,ckd->qkgd", weights.astype(jnp.float32), all_values)
    return mixed.astype(jnp.bfloat16).reshape(NEW_TOKENS, QUERY_HEADS * HEAD_SIZE)


def pick_slot(grid, slot_index):
    return jnp.take_along_axis(grid, slot_index[:, None, None, None], axis=1)[:, 0]


def reference(queries, fresh_kv, key_value_pages, cache_lengths, page_table, movers, w_out):
    owner = jnp.arange(TOTAL_REQUESTS, dtype=jnp.int32) // REQ_DEV

    def single(request):
        page_rows = owner[request] * PAGES_PER_DEVICE + page_table[request]
        page_list = jnp.take(key_value_pages, page_rows, axis=0)
        return attend_one(queries[request], fresh_kv[request], page_list, cache_lengths[request])

    attended = lax.map(single, jnp.arange(TOTAL_REQUESTS, dtype=jnp.int32))
    grid = attended.reshape(OWNING_DEVICES, REQ_DEV, NEW_TOKENS, QUERY_HEADS * HEAD_SIZE)
    to_next = movers[:, 0]
    to_prev = movers[:, 1]
    from_left = jnp.roll(pick_slot(grid, to_next), 1, axis=0)
    from_right = jnp.roll(pick_slot(grid, to_prev), -1, axis=0)
    slot_ids = jnp.arange(REQ_DEV, dtype=jnp.int32)[None, :, None, None]
    placed = jnp.where(slot_ids == to_next[:, None, None, None], from_left[:, None],
                       jnp.where(slot_ids == to_prev[:, None, None, None], from_right[:, None], grid))
    flat = placed.reshape(TOKENS, QUERY_HEADS * HEAD_SIZE)
    return jnp.dot(flat, w_out.T, preferred_element_type=jnp.float32).astype(jnp.bfloat16)
```

```python
import functools

import jax
import jax.numpy as jnp
from jax import lax
from jax.experimental import pallas as pl
from jax.experimental.pallas import tpu as pltpu
from jax.sharding import PartitionSpec as P

HEAD_SIZE = 128
PAGE_GROUP = 4
LOG2E = 1.4426950408889634
MASKED = -1e30


def passed_along(block, axis, distance):
    devices = range(lax.axis_size(axis))
    route = [((i - distance) % len(devices), i) for i in devices]
    return lax.ppermute(block, axis, route)


def nt(a, b):
    return lax.dot_general(a, b, (((1,), (1,)), ((), ())), preferred_element_type=jnp.float32)


def attend_kernel(kv_heads, group, len_ref, tab_ref, q_ref, f_ref, pages_ref, o_ref, qs, ms, ls, acc):
    slot = pl.program_id(0)
    tokens = q_ref.shape[1]
    page = pages_ref.shape[1]
    rows = group * tokens
    maxp = tab_ref.shape[1]
    length = len_ref[slot]
    factor = HEAD_SIZE ** (-0.5) * LOG2E
    span = PAGE_GROUP * page
    groups = (length + span - 1) // span
    token = lax.broadcasted_iota(jnp.int32, (rows, tokens), 0) % tokens
    newer = lax.broadcasted_iota(jnp.int32, (rows, tokens), 1)
    for g in range(kv_heads):
        heads = [
            q_ref[0, :, (g * group + h) * HEAD_SIZE : (g * group + h + 1) * HEAD_SIZE].astype(jnp.float32)
            for h in range(group)
        ]
        q = jnp.concatenate(heads, axis=0).astype(jnp.bfloat16)
        qs[g] = q
        key = f_ref[0, :, 2 * g * HEAD_SIZE : (2 * g + 1) * HEAD_SIZE]
        value = f_ref[0, :, (2 * g + 1) * HEAD_SIZE : (2 * g + 2) * HEAD_SIZE]
        s = jnp.where(newer <= token, nt(q, key), MASKED)
        m = jnp.max(s, axis=-1, keepdims=True)
        p = jnp.exp2((s - m) * factor)
        ms[g] = m
        ls[g] = jnp.sum(p, axis=-1, keepdims=True)
        acc[g] = jnp.dot(p.astype(jnp.bfloat16), value, preferred_element_type=jnp.float32)

    def body(at, carry):
        ids = [tab_ref[slot, jnp.minimum(at * PAGE_GROUP + u, maxp - 1)] for u in range(PAGE_GROUP)]
        pos = at * span + lax.broadcasted_iota(jnp.int32, (rows, span), 1)
        valid = pos < length
        for g in range(kv_heads):
            keys = jnp.concatenate(
                [pages_ref[i, :, 2 * g * HEAD_SIZE : (2 * g + 1) * HEAD_SIZE] for i in ids], axis=0
            )
            values = jnp.concatenate(
                [pages_ref[i, :, (2 * g + 1) * HEAD_SIZE : (2 * g + 2) * HEAD_SIZE] for i in ids], axis=0
            )
            s = jnp.where(valid, nt(qs[g], keys), MASKED)
            before = ms[g]
            m = jnp.maximum(before, jnp.max(s, axis=-1, keepdims=True))
            fade = jnp.exp2((before - m) * factor)
            p = jnp.exp2((s - m) * factor)
            ms[g] = m
            ls[g] = ls[g] * fade + jnp.sum(p, axis=-1, keepdims=True)
            acc[g] = acc[g] * fade + jnp.dot(
                p.astype(jnp.bfloat16), values, preferred_element_type=jnp.float32
            )
        return carry

    lax.fori_loop(0, groups, body, 0)
    for g in range(kv_heads):
        o = acc[g] / ls[g]
        for h in range(group):
            o_ref[0, :, (g * group + h) * HEAD_SIZE : (g * group + h + 1) * HEAD_SIZE] = o[
                h * tokens : (h + 1) * tokens
            ].astype(jnp.bfloat16)


def attend(queries, fresh_kv, pages, lengths, table):
    slots, tokens, width = queries.shape
    kv_heads = fresh_kv.shape[2] // (2 * HEAD_SIZE)
    group = width // (kv_heads * HEAD_SIZE)
    rows = group * tokens
    return pl.pallas_call(
        functools.partial(attend_kernel, kv_heads, group),
        out_shape=jax.ShapeDtypeStruct(queries.shape, jnp.bfloat16),
        grid_spec=pltpu.PrefetchScalarGridSpec(
            num_scalar_prefetch=2,
            grid=(slots,),
            in_specs=[
                pl.BlockSpec((1, tokens, width), lambda s, a, b: (s, 0, 0)),
                pl.BlockSpec((1, tokens, fresh_kv.shape[2]), lambda s, a, b: (s, 0, 0)),
                pl.BlockSpec(pages.shape, lambda s, a, b: (0, 0, 0), pipeline_mode=pl.Buffered(1)),
            ],
            out_specs=pl.BlockSpec((1, tokens, width), lambda s, a, b: (s, 0, 0)),
            scratch_shapes=[
                pltpu.VMEM((kv_heads, rows, HEAD_SIZE), jnp.bfloat16),
                pltpu.VMEM((kv_heads, rows, 1), jnp.float32),
                pltpu.VMEM((kv_heads, rows, 1), jnp.float32),
                pltpu.VMEM((kv_heads, rows, HEAD_SIZE), jnp.float32),
            ],
        ),
        compiler_params=pltpu.CompilerParams(vmem_limit_bytes=40 << 20),
        cost_estimate=pl.CostEstimate(
            flops=4 * rows * kv_heads * pages.shape[0] * pages.shape[1] * HEAD_SIZE,
            transcendentals=rows * kv_heads * pages.shape[0] * pages.shape[1],
            bytes_accessed=pages.size * 2 + queries.size * 4,
        ),
    )(lengths, table, queries, fresh_kv, pages)


def per_device(queries, fresh_kv, key_value_pages, cache_lengths, page_table, movers, w_out):
    slots, tokens, width = queries.shape
    to_next = movers[0, 0]
    to_prev = movers[0, 1]
    attended = attend(queries, fresh_kv, key_value_pages, cache_lengths, page_table)
    from_left = passed_along(attended[to_next], "req", 1)
    from_right = passed_along(attended[to_prev], "req", -1)
    slot_ids = jnp.arange(slots, dtype=jnp.int32)[:, None, None]
    placed = jnp.where(
        slot_ids == to_next, from_left[None], jnp.where(slot_ids == to_prev, from_right[None], attended)
    )
    flat = placed.reshape(slots * tokens, width)
    partial_sum = lax.dot_general(
        flat,
        lax.all_gather(w_out, "req", axis=0, tiled=True),
        (((1,), (1,)), ((), ())),
        preferred_element_type=jnp.float32,
    )
    return lax.psum_scatter(partial_sum, "tp", scatter_dimension=1, tiled=True).astype(jnp.bfloat16)


def solution(mesh):
    return jax.shard_map(
        per_device,
        mesh=mesh,
        in_specs=(
            P("req", None, "tp"),
            P("req", None, "tp"),
            P("req", None, "tp"),
            P("req"),
            P("req", None),
            P("req", None),
            P("req", "tp"),
        ),
        out_specs=P("req", "tp"),
        check_vma=False,
    )
```

```python
import functools

import jax
import jax.numpy as jnp
from jax import lax
from jax.experimental import pallas as pl
from jax.experimental.pallas import tpu as pltpu
from jax.sharding import PartitionSpec as P

HEAD_SIZE = 128
PAGE_GROUP = 4
LOG2E = 1.4426950408889634
MASKED = -1e30


def passed_along(block, axis, distance):
    devices = range(lax.axis_size(axis))
    route = [((i - distance) % len(devices), i) for i in devices]
    return lax.ppermute(block, axis, route)


def nt(a, b):
    return lax.dot_general(a, b, (((1,), (1,)), ((), ())), preferred_element_type=jnp.float32)


def attend_kernel(kv_heads, group, len_ref, tab_ref, q_ref, f_ref, pages_ref, o_ref, qs, ms, ls, acc):
    slot = pl.program_id(0)
    tokens = q_ref.shape[1]
    page = pages_ref.shape[1]
    rows = group * tokens
    maxp = tab_ref.shape[1]
    length = len_ref[slot]
    factor = HEAD_SIZE ** (-0.5) * LOG2E
    span = PAGE_GROUP * page
    groups = (length + span - 1) // span
    token = lax.broadcasted_iota(jnp.int32, (rows, tokens), 0) % tokens
    newer = lax.broadcasted_iota(jnp.int32, (rows, tokens), 1)
    for g in range(kv_heads):
        heads = [
            q_ref[0, :, (g * group + h) * HEAD_SIZE : (g * group + h + 1) * HEAD_SIZE].astype(jnp.float32)
            for h in range(group)
        ]
        q = jnp.concatenate(heads, axis=0).astype(jnp.bfloat16)
        qs[g] = q
        key = f_ref[0, :, 2 * g * HEAD_SIZE : (2 * g + 1) * HEAD_SIZE]
        value = f_ref[0, :, (2 * g + 1) * HEAD_SIZE : (2 * g + 2) * HEAD_SIZE]
        s = jnp.where(newer <= token, nt(q, key), MASKED)
        m = jnp.max(s, axis=-1, keepdims=True)
        p = jnp.exp2((s - m) * factor)
        ms[g] = m
        ls[g] = jnp.sum(p, axis=-1, keepdims=True)
        acc[g] = jnp.dot(p.astype(jnp.bfloat16), value, preferred_element_type=jnp.float32)

    def body(at, carry):
        ids = [tab_ref[slot, jnp.minimum(at * PAGE_GROUP + u, maxp - 1)] for u in range(PAGE_GROUP)]
        pos = at * span + lax.broadcasted_iota(jnp.int32, (rows, span), 1)
        valid = pos < length
        for g in range(kv_heads):
            keys = jnp.concatenate(
                [pages_ref[i, :, 2 * g * HEAD_SIZE : (2 * g + 1) * HEAD_SIZE] for i in ids], axis=0
            )
            values = jnp.concatenate(
                [pages_ref[i, :, (2 * g + 1) * HEAD_SIZE : (2 * g + 2) * HEAD_SIZE] for i in ids], axis=0
            )
            s = jnp.where(valid, nt(qs[g], keys), MASKED)
            before = ms[g]
            m = jnp.maximum(before, jnp.max(s, axis=-1, keepdims=True))
            fade = jnp.exp2((before - m) * factor)
            p = jnp.exp2((s - m) * factor)
            ms[g] = m
            ls[g] = ls[g] * fade + jnp.sum(p, axis=-1, keepdims=True)
            acc[g] = acc[g] * fade + jnp.dot(
                p.astype(jnp.bfloat16), values, preferred_element_type=jnp.float32
            )
        return carry

    lax.fori_loop(0, groups, body, 0)
    for g in range(kv_heads):
        o = acc[g] / ls[g]
        for h in range(group):
            o_ref[0, :, (g * group + h) * HEAD_SIZE : (g * group + h + 1) * HEAD_SIZE] = o[
                h * tokens : (h + 1) * tokens
            ].astype(jnp.bfloat16)


def attend(queries, fresh_kv, pages, lengths, table):
    slots, tokens, width = queries.shape
    kv_heads = fresh_kv.shape[2] // (2 * HEAD_SIZE)
    group = width // (kv_heads * HEAD_SIZE)
    rows = group * tokens
    return pl.pallas_call(
        functools.partial(attend_kernel, kv_heads, group),
        out_shape=jax.ShapeDtypeStruct(queries.shape, jnp.bfloat16),
        grid_spec=pltpu.PrefetchScalarGridSpec(
            num_scalar_prefetch=2,
            grid=(slots,),
            in_specs=[
                pl.BlockSpec((1, tokens, width), lambda s, a, b: (s, 0, 0)),
                pl.BlockSpec((1, tokens, fresh_kv.shape[2]), lambda s, a, b: (s, 0, 0)),
                pl.BlockSpec(pages.shape, lambda s, a, b: (0, 0, 0), pipeline_mode=pl.Buffered(1)),
            ],
            out_specs=pl.BlockSpec((1, tokens, width), lambda s, a, b: (s, 0, 0)),
            scratch_shapes=[
                pltpu.VMEM((kv_heads, rows, HEAD_SIZE), jnp.bfloat16),
                pltpu.VMEM((kv_heads, rows, 1), jnp.float32),
                pltpu.VMEM((kv_heads, rows, 1), jnp.float32),
                pltpu.VMEM((kv_heads, rows, HEAD_SIZE), jnp.float32),
            ],
        ),
        compiler_params=pltpu.CompilerParams(vmem_limit_bytes=40 << 20),
        cost_estimate=pl.CostEstimate(
            flops=4 * rows * kv_heads * pages.shape[0] * pages.shape[1] * HEAD_SIZE,
            transcendentals=rows * kv_heads * pages.shape[0] * pages.shape[1],
            bytes_accessed=pages.size * 2 + queries.size * 4,
        ),
    )(lengths, table, queries, fresh_kv, pages)

CHUNKS = 4
MESH = pl.DeviceIdType.MESH


def project_kernel(
    n, a_ref, w_ref, o_ref, buf, part, theirs, summed, out,
    ring_send, ring_recv, twin_send, twin_recv, x_send, x_recv, o_send, o_recv,
):
    me, t = lax.axis_index("req"), lax.axis_index("tp")
    other = 1 - t
    chips, cols = n // 2, n // 2
    half = chips // 2
    core, chip = me % 2, me // 2
    twin = me + 1 - 2 * core
    z, y = chip // 2, chip % 2
    at = z + y * (chips - 1 - 2 * z)
    wide = w_ref.shape[0]
    depth = w_ref.shape[1] // CHUNKS

    def owner(place, which):
        place = (place + 2 * chips) % chips
        far = place // half
        return 2 * (2 * (place + far * (chips - 1 - 2 * place)) + far) + which

    def place_of(step, side):
        return at - step * (1 - 2 * side)

    my_index = me * 2 + t

    barrier = pltpu.get_barrier_semaphore()

    def greet(i, carry):
        target = (my_index + i) % (2 * n)
        pl.semaphore_signal(
            barrier, inc=1, device_id={"req": target // 2, "tp": target % 2}, device_id_type=MESH
        )
        return carry

    lax.fori_loop(1, 2 * n, greet, 0)
    buf[me] = a_ref[...]
    pl.semaphore_wait(barrier, 2 * n - 1)

    def ring_copy(step, side, c):
        where = buf.at[owner(place_of(step, side), core), side, :, pl.ds(c * depth, depth)]
        return pltpu.make_async_remote_copy(
            src_ref=where, dst_ref=where,
            send_sem=ring_send.at[step, side, c], recv_sem=ring_recv.at[step, side, c],
            device_id={"req": owner(at + 1 - 2 * side, core), "tp": t}, device_id_type=MESH,
        )

    def ring_arrival(step, side, c):
        where = buf.at[owner(place_of(step + 1, side), core), side, :, pl.ds(c * depth, depth)]
        return pltpu.make_async_remote_copy(
            src_ref=where, dst_ref=where,
            send_sem=ring_send.at[step, side, c], recv_sem=ring_recv.at[step, side, c],
            device_id={"req": owner(at + 1 - 2 * side, core), "tp": t}, device_id_type=MESH,
        )

    def twin_copy(step, side, which):
        where = buf.at[owner(place_of(step, side), which), side]
        return pltpu.make_async_remote_copy(
            src_ref=where, dst_ref=where,
            send_sem=twin_send.at[step, side], recv_sem=twin_recv.at[step, side],
            device_id={"req": twin, "tp": t}, device_id_type=MESH,
        )

    def x_copy(o):
        return pltpu.make_async_remote_copy(
            src_ref=part.at[o, other], dst_ref=theirs.at[o],
            send_sem=x_send.at[o], recv_sem=x_recv.at[o],
            device_id={"req": me, "tp": other}, device_id_type=MESH,
        )

    dest_tp, dest_col = me // cols, me % cols

    def out_copy(o):
        return pltpu.make_async_remote_copy(
            src_ref=summed.at[o],
            dst_ref=out.at[t, :, pl.ds(pl.multiple_of(dest_col * wide, wide), wide)],
            send_sem=o_send.at[o], recv_sem=o_recv.at[t, dest_col],
            device_id={"req": o, "tp": dest_tp}, device_id_type=MESH,
        )

    def multiply(o, side):
        part[o, side] = nt(buf[o, side], w_ref[...])

    def reduce(o):
        x_copy(o).wait_recv()
        summed[o] = (part[o, t] + theirs[o]).astype(jnp.bfloat16)

    for c in range(CHUNKS):
        for side in range(2):
            ring_copy(0, side, c).start()
    for side in range(2):
        twin_copy(0, side, core).start()
    for side in range(2):
        multiply(me, side)
    x_copy(me).start()

    def step_body(step, carry):
        for c in range(CHUNKS):
            for side in range(2):
                ring_arrival(step - 1, side, c).wait_recv()

                @pl.when(step < chips - 1)
                def _():
                    ring_copy(step, side, c).start()

        for side in range(2):
            twin_copy(step, side, core).start()
        for side in range(2):
            multiply(owner(place_of(step, side), core), side)
        x_copy(owner(place_of(step, other), core)).start()
        for side in range(2):
            twin_copy(step - 1, side, 1 - core).wait_recv()
            multiply(owner(place_of(step - 1, side), 1 - core), side)
        x_copy(owner(place_of(step - 1, other), 1 - core)).start()

        @pl.when(step >= 2)
        def _():
            mine = owner(place_of(step - 1, t), core)
            reduce(mine)
            out_copy(mine).start()
            twins = owner(place_of(step - 2, t), 1 - core)
            reduce(twins)
            out_copy(twins).start()

        return carry

    lax.fori_loop(1, chips, step_body, 0)

    for side in range(2):
        twin_copy(chips - 1, side, 1 - core).wait_recv()
        multiply(owner(place_of(chips - 1, side), 1 - core), side)
    x_copy(owner(place_of(chips - 1, other), 1 - core)).start()

    reduce(me)

    @pl.when(dest_tp == t)
    def _():
        out[t, :, pl.ds(pl.multiple_of(dest_col * wide, wide), wide)] = summed[me]

    @pl.when(dest_tp != t)
    def _():
        out_copy(me).start()

    for o in (
        owner(place_of(chips - 1, t), core),
        owner(place_of(chips - 2, t), 1 - core),
        owner(place_of(chips - 1, t), 1 - core),
    ):
        reduce(o)
        out_copy(o).start()

    def ring_done(step, carry):
        for side in range(2):
            for c in range(CHUNKS):
                ring_copy(step, side, c).wait_send()
        return carry

    def twin_done(step, carry):
        for side in range(2):
            twin_copy(step, side, core).wait_send()
        return carry

    def x_done(o, carry):
        x_copy(o).wait_send()

        @pl.when(jnp.logical_or(o != me, dest_tp != t))
        def _():
            out_copy(o).wait_send()

        return carry

    lax.fori_loop(0, chips - 1, ring_done, 0)
    lax.fori_loop(0, chips, twin_done, 0)
    lax.fori_loop(0, n, x_done, 0)

    def arrived(j, carry):
        for h in range(2):
            @pl.when(jnp.logical_or(t * cols + j != me, t != h))
            def _():
                where = out.at[h, :, pl.ds(pl.multiple_of(j * wide, wide), wide)]
                pltpu.make_async_remote_copy(
                    src_ref=summed.at[0], dst_ref=where,
                    send_sem=o_send.at[0], recv_sem=o_recv.at[h, j],
                    device_id={"req": twin, "tp": t}, device_id_type=MESH,
                ).wait_recv()

        return carry

    lax.fori_loop(0, cols, arrived, 0)
    o_ref[...] = out[...]


def project(flat, w_out):
    n = lax.axis_size("req")
    rows, width = flat.shape
    wide = w_out.shape[0]
    side, cols = rows // 2, n // 2
    dma = pltpu.SemaphoreType.DMA
    vmem = pl.BlockSpec(memory_space=pltpu.VMEM)
    done = pl.pallas_call(
        functools.partial(project_kernel, n),
        out_shape=jax.ShapeDtypeStruct((2, side, cols * wide), jnp.bfloat16),
        in_specs=[vmem, vmem],
        out_specs=vmem,
        scratch_shapes=[
            pltpu.VMEM((n, 2, side, width), jnp.bfloat16),
            pltpu.VMEM((n, 2, side, wide), jnp.float32),
            pltpu.VMEM((n, side, wide), jnp.float32),
            pltpu.VMEM((n, side, wide), jnp.bfloat16),
            pltpu.VMEM((2, side, cols * wide), jnp.bfloat16),
            dma((cols - 1, 2, CHUNKS)),
            dma((cols - 1, 2, CHUNKS)),
            dma((cols, 2)),
            dma((cols, 2)),
            dma((n,)),
            dma((n,)),
            dma((n,)),
            dma((2, cols)),
        ],
        compiler_params=pltpu.CompilerParams(
            collective_id=0, has_side_effects=True, vmem_limit_bytes=48 << 20
        ),
    )(flat.reshape(2, side, width), w_out)
    return done.reshape(rows, cols * wide)


def per_device(queries, fresh_kv, key_value_pages, cache_lengths, page_table, movers, w_out):
    slots, tokens, width = queries.shape
    to_next = movers[0, 0]
    to_prev = movers[0, 1]
    attended = attend(queries, fresh_kv, key_value_pages, cache_lengths, page_table)
    from_left = passed_along(attended[to_next], "req", 1)
    from_right = passed_along(attended[to_prev], "req", -1)
    slot_ids = jnp.arange(slots, dtype=jnp.int32)[:, None, None]
    placed = jnp.where(
        slot_ids == to_next, from_left[None], jnp.where(slot_ids == to_prev, from_right[None], attended)
    )
    flat = placed.reshape(slots * tokens, width)
    if lax.axis_size("tp") == 2 and lax.axis_size("req") % 4 == 0:
        return project(flat, w_out)
    partial_sum = lax.dot_general(
        flat,
        lax.all_gather(w_out, "req", axis=0, tiled=True),
        (((1,), (1,)), ((), ())),
        preferred_element_type=jnp.float32,
    )
    return lax.psum_scatter(partial_sum, "tp", scatter_dimension=1, tiled=True).astype(jnp.bfloat16)


def solution(mesh):
    return jax.shard_map(
        per_device,
        mesh=mesh,
        in_specs=(
            P("req", None, "tp"),
            P("req", None, "tp"),
            P("req", None, "tp"),
            P("req"),
            P("req", None),
            P("req", None),
            P("req", "tp"),
        ),
        out_specs=P("req", "tp"),
        check_vma=False,
    )
```

```python
import functools

import jax
import jax.numpy as jnp
from jax import lax
from jax.experimental import pallas as pl
from jax.experimental.pallas import tpu as pltpu
from jax.sharding import PartitionSpec as P

HEAD_SIZE = 128
PAGE_GROUP = 8
LOG2E = 1.4426950408889634
MASKED = -1e30


def passed_along(block, axis, distance):
    devices = range(lax.axis_size(axis))
    route = [((i - distance) % len(devices), i) for i in devices]
    return lax.ppermute(block, axis, route)


def nt(a, b):
    return lax.dot_general(a, b, (((1,), (1,)), ((), ())), preferred_element_type=jnp.float32)


def attend_kernel(kv_heads, group, len_ref, tab_ref, q_ref, f_ref, pages_ref, o_ref, qs, ms, ls, acc):
    slot = pl.program_id(0)
    tokens = q_ref.shape[1]
    page = pages_ref.shape[1]
    rows = group * tokens
    maxp = tab_ref.shape[1]
    length = len_ref[slot]
    factor = HEAD_SIZE ** (-0.5) * LOG2E
    span = PAGE_GROUP * page
    groups = (length + span - 1) // span
    token = lax.broadcasted_iota(jnp.int32, (rows, tokens), 0) % tokens
    newer = lax.broadcasted_iota(jnp.int32, (rows, tokens), 1)
    for g in range(kv_heads):
        heads = [
            q_ref[0, :, (g * group + h) * HEAD_SIZE : (g * group + h + 1) * HEAD_SIZE].astype(jnp.float32)
            for h in range(group)
        ]
        q = jnp.concatenate(heads, axis=0).astype(jnp.bfloat16)
        qs[g] = q
        key = f_ref[0, :, 2 * g * HEAD_SIZE : (2 * g + 1) * HEAD_SIZE]
        value = f_ref[0, :, (2 * g + 1) * HEAD_SIZE : (2 * g + 2) * HEAD_SIZE]
        s = jnp.where(newer <= token, nt(q, key), MASKED)
        m = jnp.max(s, axis=-1, keepdims=True)
        p = jnp.exp2((s - m) * factor)
        ms[g] = m
        ls[g] = jnp.sum(p, axis=-1, keepdims=True)
        acc[g] = jnp.dot(p.astype(jnp.bfloat16), value, preferred_element_type=jnp.float32)

    def body(at, carry):
        ids = [tab_ref[slot, jnp.minimum(at * PAGE_GROUP + u, maxp - 1)] for u in range(PAGE_GROUP)]
        pos = at * span + lax.broadcasted_iota(jnp.int32, (rows, span), 1)
        valid = pos < length
        def side(g, which):
            first = (2 * g + which) * HEAD_SIZE
            return jnp.concatenate([pages_ref[i, :, first : first + HEAD_SIZE] for i in ids], axis=0)

        def scored(g):
            return jnp.where(valid, nt(qs[g], side(g, 0)), MASKED)

        s = scored(0)
        for g in range(kv_heads):
            following = scored(g + 1) if g + 1 < kv_heads else None
            before = ms[g]
            m = jnp.maximum(before, jnp.max(s, axis=-1, keepdims=True))
            fade = jnp.exp2((before - m) * factor)
            p = jnp.exp2((s - m) * factor)
            ms[g] = m
            ls[g] = ls[g] * fade + jnp.sum(p, axis=-1, keepdims=True)
            acc[g] = acc[g] * fade + jnp.dot(
                p.astype(jnp.bfloat16), side(g, 1), preferred_element_type=jnp.float32
            )
            s = following
        return carry

    lax.fori_loop(0, groups, body, 0)
    for g in range(kv_heads):
        o = acc[g] / ls[g]
        for h in range(group):
            o_ref[0, :, (g * group + h) * HEAD_SIZE : (g * group + h + 1) * HEAD_SIZE] = o[
                h * tokens : (h + 1) * tokens
            ].astype(jnp.bfloat16)


def attend(queries, fresh_kv, pages, lengths, table):
    slots, tokens, width = queries.shape
    kv_heads = fresh_kv.shape[2] // (2 * HEAD_SIZE)
    group = width // (kv_heads * HEAD_SIZE)
    rows = group * tokens
    return pl.pallas_call(
        functools.partial(attend_kernel, kv_heads, group),
        out_shape=jax.ShapeDtypeStruct(queries.shape, jnp.bfloat16),
        grid_spec=pltpu.PrefetchScalarGridSpec(
            num_scalar_prefetch=2,
            grid=(slots,),
            in_specs=[
                pl.BlockSpec((1, tokens, width), lambda s, a, b: (s, 0, 0)),
                pl.BlockSpec((1, tokens, fresh_kv.shape[2]), lambda s, a, b: (s, 0, 0)),
                pl.BlockSpec(pages.shape, lambda s, a, b: (0, 0, 0), pipeline_mode=pl.Buffered(1)),
            ],
            out_specs=pl.BlockSpec((1, tokens, width), lambda s, a, b: (s, 0, 0)),
            scratch_shapes=[
                pltpu.VMEM((kv_heads, rows, HEAD_SIZE), jnp.bfloat16),
                pltpu.VMEM((kv_heads, rows, 1), jnp.float32),
                pltpu.VMEM((kv_heads, rows, 1), jnp.float32),
                pltpu.VMEM((kv_heads, rows, HEAD_SIZE), jnp.float32),
            ],
        ),
        compiler_params=pltpu.CompilerParams(vmem_limit_bytes=40 << 20),
        cost_estimate=pl.CostEstimate(
            flops=4 * rows * kv_heads * pages.shape[0] * pages.shape[1] * HEAD_SIZE,
            transcendentals=rows * kv_heads * pages.shape[0] * pages.shape[1],
            bytes_accessed=pages.size * 2 + queries.size * 4,
        ),
    )(lengths, table, queries, fresh_kv, pages)

CHUNKS = 4
MESH = pl.DeviceIdType.MESH


def project_kernel(
    n, a_ref, w_ref, o_ref, buf, part, theirs, summed, out,
    ring_send, ring_recv, twin_send, twin_recv, x_send, x_recv, o_send, o_recv,
):
    me, t = lax.axis_index("req"), lax.axis_index("tp")
    other = 1 - t
    chips, cols = n // 2, n // 2
    half = chips // 2
    core, chip = me % 2, me // 2
    twin = me + 1 - 2 * core
    z, y = chip // 2, chip % 2
    at = z + y * (chips - 1 - 2 * z)
    wide = w_ref.shape[0]
    depth = w_ref.shape[1] // CHUNKS

    def owner(place, which):
        place = (place + 2 * chips) % chips
        far = place // half
        return 2 * (2 * (place + far * (chips - 1 - 2 * place)) + far) + which

    def place_of(step, side):
        return at - step * (1 - 2 * side)

    my_index = me * 2 + t

    barrier = pltpu.get_barrier_semaphore()

    def greet(i, carry):
        target = (my_index + i) % (2 * n)
        pl.semaphore_signal(
            barrier, inc=1, device_id={"req": target // 2, "tp": target % 2}, device_id_type=MESH
        )
        return carry

    lax.fori_loop(1, 2 * n, greet, 0)
    buf[me] = a_ref[...]
    pl.semaphore_wait(barrier, 2 * n - 1)

    def ring_copy(step, side, c):
        where = buf.at[owner(place_of(step, side), core), side, :, pl.ds(c * depth, depth)]
        return pltpu.make_async_remote_copy(
            src_ref=where, dst_ref=where,
            send_sem=ring_send.at[step, side, c], recv_sem=ring_recv.at[step, side, c],
            device_id={"req": owner(at + 1 - 2 * side, core), "tp": t}, device_id_type=MESH,
        )

    def ring_arrival(step, side, c):
        where = buf.at[owner(place_of(step + 1, side), core), side, :, pl.ds(c * depth, depth)]
        return pltpu.make_async_remote_copy(
            src_ref=where, dst_ref=where,
            send_sem=ring_send.at[step, side, c], recv_sem=ring_recv.at[step, side, c],
            device_id={"req": owner(at + 1 - 2 * side, core), "tp": t}, device_id_type=MESH,
        )

    def twin_copy(step, side, which):
        where = buf.at[owner(place_of(step, side), which), side]
        return pltpu.make_async_remote_copy(
            src_ref=where, dst_ref=where,
            send_sem=twin_send.at[step, side], recv_sem=twin_recv.at[step, side],
            device_id={"req": twin, "tp": t}, device_id_type=MESH,
        )

    def x_copy(o):
        return pltpu.make_async_remote_copy(
            src_ref=part.at[o, other], dst_ref=theirs.at[o],
            send_sem=x_send.at[o], recv_sem=x_recv.at[o],
            device_id={"req": me, "tp": other}, device_id_type=MESH,
        )

    dest_tp, dest_col = me // cols, me % cols

    def out_copy(o):
        return pltpu.make_async_remote_copy(
            src_ref=summed.at[o],
            dst_ref=out.at[t, :, pl.ds(pl.multiple_of(dest_col * wide, wide), wide)],
            send_sem=o_send.at[o], recv_sem=o_recv.at[t, dest_col],
            device_id={"req": o, "tp": dest_tp}, device_id_type=MESH,
        )

    def multiply(o, side):
        part[o, side] = nt(buf[o, side], w_ref[...])

    def reduce(o):
        x_copy(o).wait_recv()
        summed[o] = (part[o, t] + theirs[o]).astype(jnp.bfloat16)

    for c in range(CHUNKS):
        for side in range(2):
            ring_copy(0, side, c).start()
    for side in range(2):
        twin_copy(0, side, core).start()
    for side in range(2):
        multiply(me, side)
    x_copy(me).start()

    def step_body(step, carry):
        for c in range(CHUNKS):
            for side in range(2):
                ring_arrival(step - 1, side, c).wait_recv()

                @pl.when(step < chips - 1)
                def _():
                    ring_copy(step, side, c).start()

        for side in range(2):
            twin_copy(step, side, core).start()
        for side in range(2):
            multiply(owner(place_of(step, side), core), side)
        x_copy(owner(place_of(step, other), core)).start()
        for side in range(2):
            twin_copy(step - 1, side, 1 - core).wait_recv()
            multiply(owner(place_of(step - 1, side), 1 - core), side)
        x_copy(owner(place_of(step - 1, other), 1 - core)).start()

        @pl.when(step >= 2)
        def _():
            mine = owner(place_of(step - 1, t), core)
            reduce(mine)
            out_copy(mine).start()
            twins = owner(place_of(step - 2, t), 1 - core)
            reduce(twins)
            out_copy(twins).start()

        return carry

    lax.fori_loop(1, chips, step_body, 0)

    for side in range(2):
        twin_copy(chips - 1, side, 1 - core).wait_recv()
        multiply(owner(place_of(chips - 1, side), 1 - core), side)
    x_copy(owner(place_of(chips - 1, other), 1 - core)).start()

    reduce(me)

    @pl.when(dest_tp == t)
    def _():
        out[t, :, pl.ds(pl.multiple_of(dest_col * wide, wide), wide)] = summed[me]

    @pl.when(dest_tp != t)
    def _():
        out_copy(me).start()

    for o in (
        owner(place_of(chips - 1, t), core),
        owner(place_of(chips - 2, t), 1 - core),
        owner(place_of(chips - 1, t), 1 - core),
    ):
        reduce(o)
        out_copy(o).start()

    def ring_done(step, carry):
        for side in range(2):
            for c in range(CHUNKS):
                ring_copy(step, side, c).wait_send()
        return carry

    def twin_done(step, carry):
        for side in range(2):
            twin_copy(step, side, core).wait_send()
        return carry

    def x_done(o, carry):
        x_copy(o).wait_send()

        @pl.when(jnp.logical_or(o != me, dest_tp != t))
        def _():
            out_copy(o).wait_send()

        return carry

    lax.fori_loop(0, chips - 1, ring_done, 0)
    lax.fori_loop(0, chips, twin_done, 0)
    lax.fori_loop(0, n, x_done, 0)

    def arrived(j, carry):
        for h in range(2):
            @pl.when(jnp.logical_or(t * cols + j != me, t != h))
            def _():
                where = out.at[h, :, pl.ds(pl.multiple_of(j * wide, wide), wide)]
                pltpu.make_async_remote_copy(
                    src_ref=summed.at[0], dst_ref=where,
                    send_sem=o_send.at[0], recv_sem=o_recv.at[h, j],
                    device_id={"req": twin, "tp": t}, device_id_type=MESH,
                ).wait_recv()

        return carry

    lax.fori_loop(0, cols, arrived, 0)
    o_ref[...] = out[...]


def project(flat, w_out):
    n = lax.axis_size("req")
    rows, width = flat.shape
    wide = w_out.shape[0]
    side, cols = rows // 2, n // 2
    dma = pltpu.SemaphoreType.DMA
    vmem = pl.BlockSpec(memory_space=pltpu.VMEM)
    done = pl.pallas_call(
        functools.partial(project_kernel, n),
        out_shape=jax.ShapeDtypeStruct((2, side, cols * wide), jnp.bfloat16),
        in_specs=[vmem, vmem],
        out_specs=vmem,
        scratch_shapes=[
            pltpu.VMEM((n, 2, side, width), jnp.bfloat16),
            pltpu.VMEM((n, 2, side, wide), jnp.float32),
            pltpu.VMEM((n, side, wide), jnp.float32),
            pltpu.VMEM((n, side, wide), jnp.bfloat16),
            pltpu.VMEM((2, side, cols * wide), jnp.bfloat16),
            dma((cols - 1, 2, CHUNKS)),
            dma((cols - 1, 2, CHUNKS)),
            dma((cols, 2)),
            dma((cols, 2)),
            dma((n,)),
            dma((n,)),
            dma((n,)),
            dma((2, cols)),
        ],
        compiler_params=pltpu.CompilerParams(
            collective_id=0, has_side_effects=True, vmem_limit_bytes=48 << 20
        ),
    )(flat.reshape(2, side, width), w_out)
    return done.reshape(rows, cols * wide)


def per_device(queries, fresh_kv, key_value_pages, cache_lengths, page_table, movers, w_out):
    slots, tokens, width = queries.shape
    to_next = movers[0, 0]
    to_prev = movers[0, 1]
    attended = attend(queries, fresh_kv, key_value_pages, cache_lengths, page_table)
    from_left = passed_along(attended[to_next], "req", 1)
    from_right = passed_along(attended[to_prev], "req", -1)
    slot_ids = jnp.arange(slots, dtype=jnp.int32)[:, None, None]
    placed = jnp.where(
        slot_ids == to_next, from_left[None], jnp.where(slot_ids == to_prev, from_right[None], attended)
    )
    flat = placed.reshape(slots * tokens, width)
    if lax.axis_size("tp") == 2 and lax.axis_size("req") % 4 == 0:
        return project(flat, w_out)
    partial_sum = lax.dot_general(
        flat,
        lax.all_gather(w_out, "req", axis=0, tiled=True),
        (((1,), (1,)), ((), ())),
        preferred_element_type=jnp.float32,
    )
    return lax.psum_scatter(partial_sum, "tp", scatter_dimension=1, tiled=True).astype(jnp.bfloat16)


def solution(mesh):
    return jax.shard_map(
        per_device,
        mesh=mesh,
        in_specs=(
            P("req", None, "tp"),
            P("req", None, "tp"),
            P("req", None, "tp"),
            P("req"),
            P("req", None),
            P("req", None),
            P("req", "tp"),
        ),
        out_specs=P("req", "tp"),
        check_vma=False,
    )
```
